32 devices in a mesh: rep: 4 (over z), fsdp: 8 (over y, x, core).
Axes of the slice: x: 2, y: 2, z: 4, core: 2. Of those that a mesh axis runs over, the one named last changes fastest.
Arguments:
- tokens: bfloat16 [4096, 3072], P(('rep', 'fsdp')), may hold values from -6 to 6
- gate_saved: bfloat16 [4096, 8192], P('rep', 'fsdp'), may hold values from -6 to 6
- up_saved: bfloat16 [4096, 8192], P('rep', 'fsdp'), may hold values from -6 to 6
- hidden_grad: bfloat16 [4096, 8192], P('rep', 'fsdp'), may hold values from -6 to 6
- gate_num: bfloat16 [4, 3072, 8192], P('rep', None, 'fsdp'), may hold values from -6 to 6
- up_num: bfloat16 [4, 3072, 8192], P('rep', None, 'fsdp'), may hold values from -6 to 6
- push_weight: bfloat16 [4], P('rep'), may hold values from 0.5 to 2
- step: int32 [1], replicated, may hold values from 0 to 15
Outputs:
- input_grad: bfloat16 [4096, 3072], P(('rep', 'fsdp'))
- gate_next: bfloat16 [4, 3072, 8192], P('rep', None, 'fsdp')
- up_next: bfloat16 [4, 3072, 8192], P('rep', None, 'fsdp')
- weight_next: float32 [4], P('rep')
The draws below stay inside these ranges and needn't reach their ends.
All inputs are finite; a program needn't handle non-finite values.
Results may differ from the reference program's by a relative error of at most 0.017.
Values may be sent and summed in bfloat16 or wider, within the bound.
A program may use at most 192 MiB of HBM per device.

```python
import math
import jax
import jax.numpy as jnp
from jax import lax

D = 3072
FF = 8192
TOK_DEV = 128
TOKENS = 4096
N_REP = 4
N_FSDP = 8


def block_levels(rng, extent, split, smallest, high):
    gain, own = 1.0, jax.random.fold_in(rng, 6)
    for axis_at, blocks in split:
        draws = jnp.exp(jax.random.uniform(jax.random.fold_in(own, axis_at), (blocks,), jnp.float32, smallest / len(split), high / len(split)))
        gain = gain * jnp.repeat(draws, extent[axis_at] // blocks).reshape([-1 if axis == axis_at else 1 for axis in range(len(extent))])
    return gain


def bell_draw(stream_key, extent, deviation, reach, split=(), held_as=jnp.bfloat16):
    result = deviation * jax.random.normal(stream_key, extent, jnp.float32)
    if split:
        result = result * block_levels(stream_key, extent, split, -0.22, 0.18)
    return jnp.clip(result, -reach, reach).astype(held_as)


def setup_inputs(seed: int = 0) -> dict:
    streams_of = jax.random.split(jax.random.key(seed), 9)
    return {
        "tokens": bell_draw(streams_of[0], (TOKENS, D), 1.0, 6.0, ((0, 32),)),
        "gate_saved": bell_draw(streams_of[1], (TOKENS, FF), 1.0, 6.0, ((0, 4), (1, 8))),
        "up_saved": bell_draw(streams_of[2], (TOKENS, FF), 1.0, 6.0, ((0, 4), (1, 8))),
        "hidden_grad": bell_draw(streams_of[3], (TOKENS, FF), 1.0, 6.0, ((0, 4), (1, 8))),
        "gate_num": bell_draw(streams_of[4], (N_REP, D, FF), 1.0, 6.0, ((0, 4), (2, 8))),
        "up_num": bell_draw(streams_of[5], (N_REP, D, FF), 1.0, 6.0, ((0, 4), (2, 8))),
        "push_weight": jnp.clip(jnp.exp(math.log(2.0) - 1.3862944 * jax.random.uniform(streams_of[6], (N_REP,), jnp.float32) ** block_levels(streams_of[6], (N_REP,), ((0, 4),), -0.2, 0.2)), 0.5, 2.0).astype(jnp.bfloat16),
        "step": jax.random.randint(streams_of[7], (1,), 0, 16).astype(jnp.int32),
    }


def reference(tokens, gate_saved, up_saved, hidden_grad, gate_num, up_num, push_weight, step):
    factor = D ** -0.5
    count_rows = TOK_DEV * N_FSDP
    block_cols = FF // N_FSDP
    levels = N_REP.bit_length() - 1

    def replica_terms(replica):
        offset = replica * count_rows
        inputs = lax.dynamic_slice_in_dim(tokens, offset, count_rows, 0)
        gate_act = lax.dynamic_slice_in_dim(gate_saved, offset, count_rows, 0).astype(jnp.float32)
        up_act = lax.dynamic_slice_in_dim(up_saved, offset, count_rows, 0).astype(jnp.float32)
        cotangent = lax.dynamic_slice_in_dim(hidden_grad, offset, count_rows, 0).astype(jnp.float32)
        weight = lax.dynamic_index_in_dim(push_weight, replica, 0, False).astype(jnp.float32)
        gate_master = lax.dynamic_index_in_dim(gate_num, replica, 0, False)
        up_master = lax.dynamic_index_in_dim(up_num, replica, 0, False)
        gate_point = (gate_master.astype(jnp.float32) / weight).astype(jnp.bfloat16)
        up_point = (up_master.astype(jnp.float32) / weight).astype(jnp.bfloat16)
        logistic = jax.nn.sigmoid(gate_act)
        gate_delta = (cotangent * up_act * logistic * (1.0 + gate_act * (1.0 - logistic))).astype(jnp.bfloat16)
        up_delta = (cotangent * gate_act * logistic).astype(jnp.bfloat16)
        gate_grad = (factor * jnp.dot(inputs.T, gate_delta, preferred_element_type=jnp.float32)).astype(jnp.bfloat16)
        up_grad = (factor * jnp.dot(inputs.T, up_delta, preferred_element_type=jnp.float32)).astype(jnp.bfloat16)
        gate_half = (gate_master.astype(jnp.float32) - gate_grad.astype(jnp.float32)).astype(jnp.bfloat16)
        up_half = (up_master.astype(jnp.float32) - up_grad.astype(jnp.float32)).astype(jnp.bfloat16)

        def add_block(total, block):
            first = (block * block_cols).astype(jnp.int32)
            gate_cols = lax.dynamic_slice_in_dim(gate_delta, first, block_cols, 1)
            up_cols = lax.dynamic_slice_in_dim(up_delta, first, block_cols, 1)
            gate_rows = lax.dynamic_slice_in_dim(gate_point, first, block_cols, 1)
            up_rows = lax.dynamic_slice_in_dim(up_point, first, block_cols, 1)
            part = factor * (jnp.dot(gate_cols, gate_rows.T, preferred_element_type=jnp.float32)
                             + jnp.dot(up_cols, up_rows.T, preferred_element_type=jnp.float32))
            return total + part.astype(jnp.bfloat16).astype(jnp.float32), None

        start = jnp.zeros((count_rows, D), jnp.float32)
        input_part, unused = lax.scan(add_block, start, jnp.arange(N_FSDP, dtype=jnp.int32))
        return input_part.astype(jnp.bfloat16), gate_half, up_half

    input_parts, gate_halves, up_halves = lax.map(replica_terms, jnp.arange(N_REP, dtype=jnp.int32))
    distance = jnp.left_shift(jnp.int32(1), (step[0] % levels).astype(jnp.int32))

    def mixture(halves):
        values = halves.astype(jnp.float32)
        return (0.5 * (values + jnp.roll(values, distance, axis=0))).astype(jnp.bfloat16)

    weights = push_weight.astype(jnp.float32)
    weight_next = 0.5 * (weights + jnp.roll(weights, distance, axis=0))
    input_grad = input_parts.reshape(N_REP * count_rows, D)
    return input_grad, mixture(gate_halves), mixture(up_halves), weight_next
```

```python
from functools import partial

import jax
import jax.numpy as jnp
from jax import lax
from jax.experimental import pallas as pl
from jax.experimental.pallas import tpu as pltpu
from jax.sharding import PartitionSpec as P

MESH = pl.DeviceIdType.MESH
ANY = pl.BlockSpec(memory_space=pl.ANY)
VMEM = pl.BlockSpec(memory_space=pltpu.VMEM)
SPLITS = (3, 4, 5, 5, 4, 2, 1)


def greet(me, n):
    barrier = pltpu.get_barrier_semaphore()
    for k in range(1, n):
        pl.semaphore_signal(
            barrier, inc=1, device_id={"fsdp": lax.rem(me + k, n)}, device_id_type=MESH
        )
    pl.semaphore_wait(barrier, n - 1)


def gather_body(n, tok, out, sems, between=None):
    send, recv, fsend, frecv, local = sems
    me = lax.axis_index("fsdp")
    rows = tok.shape[0]
    beside = me + 1 - 2 * lax.rem(me, 2)

    def block(owner):
        return out.at[pl.ds(pl.multiple_of(owner * rows, rows), rows), :]

    def remote(src, owner, s, r, target):
        return pltpu.make_async_remote_copy(
            src_ref=src,
            dst_ref=block(owner),
            send_sem=s,
            recv_sem=r,
            device_id={"fsdp": target},
            device_id_type=MESH,
        )

    greet(me, n)
    direct = []
    for k in range(1, n // 2):
        copy = remote(tok, me, send.at[k], recv.at[k], lax.rem(me + 2 * k, n))
        copy.start()
        direct.append(copy)
    near = remote(tok, me, send.at[0], recv.at[0], beside)
    near.start()
    own = pltpu.make_async_copy(tok, block(me), local.at[0])
    own.start()
    if between is not None:
        between()
    relays = []
    for k in range(1, n // 2):
        owner = lax.rem(me + n - 2 * k, n)
        remote(tok, owner, send.at[k], recv.at[k], beside).wait_recv()
        copy = remote(block(owner), owner, fsend.at[k], frecv.at[k], beside)
        copy.start()
        relays.append(copy)
    own.wait()
    near.wait_send()
    remote(tok, beside, send.at[0], recv.at[0], beside).wait_recv()
    for copy in direct:
        copy.wait_send()
    for k in range(1, n // 2):
        relays[k - 1].wait_send()
        owner = lax.rem(beside + n - 2 * k, n)
        remote(tok, owner, fsend.at[k], frecv.at[k], beside).wait_recv()


def first_kernel(n, tok, gate, up, cot, out, gate_delta, up_delta, *sems):
    rows = gate.shape[0]
    tile = min(32, rows)

    def deltas():
        @pl.loop(0, rows // tile)
        def _(i):
            at = pl.ds(pl.multiple_of(i * tile, tile), tile)
            g = gate[at, :].astype(jnp.float32)
            u = up[at, :].astype(jnp.float32)
            h = cot[at, :].astype(jnp.float32)
            p = jax.nn.sigmoid(g)
            hp = h * p
            gate_delta[at, :] = (hp * u * (1.0 + g * (1.0 - p))).astype(jnp.bfloat16)
            up_delta[at, :] = (hp * g).astype(jnp.bfloat16)

    gather_body(n, tok, out, sems, deltas)


def rest_kernel(n, tok, after, out, *sems):
    gather_body(n, tok, out, sems)


def gather_sems(n):
    return [pltpu.SemaphoreType.DMA((n // 2,))] * 4 + [pltpu.SemaphoreType.DMA((1,))]


def first_call(n, tok, gate, up, cot):
    like = jax.ShapeDtypeStruct(gate.shape, jnp.bfloat16)
    return pl.pallas_call(
        partial(first_kernel, n),
        name="first_gather",
        out_shape=(jax.ShapeDtypeStruct((n * tok.shape[0], tok.shape[1]), tok.dtype), like, like),
        in_specs=[VMEM] * 4,
        out_specs=(ANY, VMEM, VMEM),
        scratch_shapes=gather_sems(n),
        compiler_params=pltpu.CompilerParams(collective_id=0, has_side_effects=True),
    )(tok, gate, up, cot)


def rest_call(n, ident, tok, after):
    return pl.pallas_call(
        partial(rest_kernel, n),
        name="rest_gather",
        out_shape=jax.ShapeDtypeStruct((n * tok.shape[0], tok.shape[1]), tok.dtype),
        in_specs=[VMEM, ANY],
        out_specs=ANY,
        scratch_shapes=gather_sems(n),
        compiler_params=pltpu.CompilerParams(collective_id=ident, has_side_effects=True),
        cost_estimate=pl.CostEstimate(flops=0, bytes_accessed=100_000_000, transcendentals=0),
    )(tok, after)


def scatter_kernel(n, term, out, parts, send, recv):
    me = lax.axis_index("fsdp")
    rows = out.shape[0]

    def block(owner):
        return term.at[pl.ds(pl.multiple_of(owner * rows, rows), rows), :]

    greet(me, n)
    own = pltpu.make_async_copy(block(me), parts.at[0], recv.at[0])
    own.start()
    copies = []
    for k in range(1, n):
        peer = lax.rem(me + k, n)
        copy = pltpu.make_async_remote_copy(
            src_ref=block(peer),
            dst_ref=parts.at[k],
            send_sem=send.at[k],
            recv_sem=recv.at[k],
            device_id={"fsdp": peer},
            device_id_type=MESH,
        )
        copy.start()
        copies.append(copy)
    own.wait()
    for copy in copies:
        copy.wait()
    tile = min(16, rows)

    @pl.loop(0, rows // tile)
    def _(i):
        at = pl.ds(pl.multiple_of(i * tile, tile), tile)
        total = parts[0, at, :].astype(jnp.float32)
        for k in range(1, n):
            total = total + parts[k, at, :].astype(jnp.float32)
        out[at, :] = total.astype(out.dtype)


def scatter_call(n, ident, term):
    rows, cols = term.shape[0] // n, term.shape[1]
    return pl.pallas_call(
        partial(scatter_kernel, n),
        name="grad_scatter",
        out_shape=jax.ShapeDtypeStruct((rows, cols), term.dtype),
        in_specs=[ANY],
        out_specs=VMEM,
        scratch_shapes=[
            pltpu.VMEM((n, rows, cols), term.dtype),
            pltpu.SemaphoreType.DMA((n,)),
            pltpu.SemaphoreType.DMA((n,)),
        ],
        compiler_params=pltpu.CompilerParams(collective_id=ident, has_side_effects=True),
        cost_estimate=pl.CostEstimate(flops=0, bytes_accessed=200_000_000, transcendentals=0),
    )(term)


def mix_kernel(after, before, gate_own, gate_peer, up_own, up_peer, gate_out, up_out):
    for own, peer, out in ((gate_own, gate_peer, gate_out), (up_own, up_peer, up_out)):
        out[...] = (0.5 * (own[...].astype(jnp.float32) + peer[...].astype(jnp.float32))).astype(
            out.dtype
        )


def mix_first(after, gate_own, gate_peer, up_own, up_peer, gate_out, up_out):
    mix_kernel(after, None, gate_own, gate_peer, up_own, up_peer, gate_out, up_out)


def mix_next(after, g0, u0, gate_own, gate_peer, up_own, up_peer, gate_out, up_out):
    mix_kernel(after, None, gate_own, gate_peer, up_own, up_peer, gate_out, up_out)


def mix_call(after, before, whole, first, tile, parts):
    rows, cols = parts[0].shape
    part = pl.BlockSpec((tile, cols), lambda i: (i, 0))
    held = pl.BlockSpec((tile, cols), lambda i: (first // tile + i, 0))
    out = jax.ShapeDtypeStruct((whole, cols), parts[0].dtype)
    return pl.pallas_call(
        mix_first if before is None else mix_next,
        name="mix",
        grid=(rows // tile,),
        out_shape=(out, out),
        in_specs=[ANY] + ([] if before is None else [ANY, ANY]) + [part] * 4,
        out_specs=(held, held),
        input_output_aliases={} if before is None else {1: 0, 2: 1},
        cost_estimate=pl.CostEstimate(
            flops=4 * rows * cols, bytes_accessed=12 * rows * cols, transcendentals=0
        ),
    )(after, *(() if before is None else before), *parts)


def halves(shard_rows, delta, num, factor):
    total = lax.dot_general(
        shard_rows, delta, (((0,), (0,)), ((), ())), preferred_element_type=jnp.float32
    )
    grad = (factor * total).astype(jnp.bfloat16)
    return (num.astype(jnp.float32) - grad.astype(jnp.float32)).astype(jnp.bfloat16)


def exchange(args, exponent):
    tokens, gate_num, up_num, push_weight, gate_delta, up_delta, gate_first, up_first = args
    n = lax.axis_size("fsdp")
    peers = lax.axis_size("rep")
    perm = [(i, (i + (1 << exponent)) % peers) for i in range(peers)]
    depth = tokens.shape[1]
    factor = depth ** (-0.5)
    unit = depth // sum(SPLITS)
    bounds = [0]
    for share in SPLITS:
        bounds.append(bounds[-1] + share * unit)

    def send(value):
        return lax.ppermute(value, "rep", perm)

    own = [(gate_first, up_first)]
    got = [(send(gate_first), send(up_first))]
    rest = rest_call(n, 1 + 2 * exponent, tokens[:, bounds[1] :], gate_first)
    for low, high in zip(bounds[1:-1], bounds[2:]):
        rows = rest[:, low - bounds[1] : high - bounds[1]]
        own.append(
            (
                halves(rows, gate_delta, gate_num[low:high], factor),
                halves(rows, up_delta, up_num[low:high], factor),
            )
        )
        got.append((send(own[-1][0]), send(own[-1][1])))
    peer_weight = send(push_weight)
    weight = push_weight[0].astype(jnp.float32)
    gate_point = (gate_num.astype(jnp.float32) / weight).astype(jnp.bfloat16)
    up_point = (up_num.astype(jnp.float32) / weight).astype(jnp.bfloat16)
    contract_cols = (((1,), (1,)), ((), ()))
    term = factor * (
        lax.dot_general(gate_delta, gate_point, contract_cols, preferred_element_type=jnp.float32)
        + lax.dot_general(up_delta, up_point, contract_cols, preferred_element_type=jnp.float32)
    )
    input_grad = scatter_call(n, 2 + 2 * exponent, term.astype(jnp.bfloat16))
    mixed = None
    for (own_gate, own_up), (peer_gate, peer_up), low in zip(own, got, bounds):
        mixed = mix_call(
            input_grad, mixed, depth, low, unit, (own_gate, peer_gate, own_up, peer_up)
        )
    weight_next = 0.5 * (push_weight.astype(jnp.float32) + peer_weight.astype(jnp.float32))
    return input_grad, mixed[0][None], mixed[1][None], weight_next


def shards(tokens, gate_saved, up_saved, hidden_grad, gate_num, up_num, push_weight, step):
    n = lax.axis_size("fsdp")
    levels = lax.axis_size("rep").bit_length() - 1
    chosen = step[0] % levels
    depth = tokens.shape[1]
    factor = depth ** (-0.5)
    first = depth // sum(SPLITS) * SPLITS[0]
    rows, gate_delta, up_delta = first_call(
        n, tokens[:, :first], gate_saved, up_saved, hidden_grad
    )
    gate_first = halves(rows, gate_delta, gate_num[0, :first], factor)
    up_first = halves(rows, up_delta, up_num[0, :first], factor)
    args = (
        tokens, gate_num[0], up_num[0], push_weight, gate_delta, up_delta, gate_first, up_first
    )
    branches = [partial(exchange, exponent=exponent) for exponent in range(levels)]
    return lax.switch(chosen, branches, args)


def solution(mesh):
    return jax.shard_map(
        shards,
        mesh=mesh,
        in_specs=(
            P(("rep", "fsdp"), None),
            P("rep", "fsdp"),
            P("rep", "fsdp"),
            P("rep", "fsdp"),
            P("rep", None, "fsdp"),
            P("rep", None, "fsdp"),
            P("rep"),
            P(),
        ),
        out_specs=(
            P(("rep", "fsdp"), None),
            P("rep", None, "fsdp"),
            P("rep", None, "fsdp"),
            P("rep"),
        ),
        check_vma=False,
    )
```

```python
from functools import partial

import jax
import jax.numpy as jnp
from jax import lax
from jax.experimental import pallas as pl
from jax.experimental.pallas import tpu as pltpu
from jax.sharding import PartitionSpec as P


MESH = pl.DeviceIdType.MESH
ANY = pl.BlockSpec(memory_space=pl.ANY)
VMEM = pl.BlockSpec(memory_space=pltpu.VMEM)
SPLITS = (3, 5, 13, 3)


def greet(me, n):
    barrier = pltpu.get_barrier_semaphore()
    for k in range(1, n):
        pl.semaphore_signal(
            barrier, inc=1, device_id={"fsdp": lax.rem(me + k, n)}, device_id_type=MESH
        )
    pl.semaphore_wait(barrier, n - 1)


def gather_body(n, tok, out, sems, between=None):
    send, recv, fsend, frecv, local = sems
    me = lax.axis_index("fsdp")
    rows = tok.shape[0]
    beside = me + 1 - 2 * lax.rem(me, 2)

    def block(owner):
        return out.at[pl.ds(pl.multiple_of(owner * rows, rows), rows), :]

    def remote(src, owner, s, r, target):
        return pltpu.make_async_remote_copy(
            src_ref=src,
            dst_ref=block(owner),
            send_sem=s,
            recv_sem=r,
            device_id={"fsdp": target},
            device_id_type=MESH,
        )

    greet(me, n)
    direct = []
    for k in range(1, n // 2):
        copy = remote(tok, me, send.at[k], recv.at[k], lax.rem(me + 2 * k, n))
        copy.start()
        direct.append(copy)
    near = remote(tok, me, send.at[0], recv.at[0], beside)
    near.start()
    own = pltpu.make_async_copy(tok, block(me), local.at[0])
    own.start()
    if between is not None:
        between()
    relays = []
    for k in range(1, n // 2):
        owner = lax.rem(me + n - 2 * k, n)
        remote(tok, owner, send.at[k], recv.at[k], beside).wait_recv()
        copy = remote(block(owner), owner, fsend.at[k], frecv.at[k], beside)
        copy.start()
        relays.append(copy)
    own.wait()
    near.wait_send()
    remote(tok, beside, send.at[0], recv.at[0], beside).wait_recv()
    for copy in direct:
        copy.wait_send()
    for k in range(1, n // 2):
        relays[k - 1].wait_send()
        owner = lax.rem(beside + n - 2 * k, n)
        remote(tok, owner, fsend.at[k], frecv.at[k], beside).wait_recv()


def first_kernel(n, tok, gate, up, cot, out, gate_delta, up_delta, *sems):
    rows = gate.shape[0]
    tile = min(32, rows)

    def deltas():
        @pl.loop(0, rows // tile)
        def _(i):
            at = pl.ds(pl.multiple_of(i * tile, tile), tile)
            g = gate[at, :].astype(jnp.float32)
            u = up[at, :].astype(jnp.float32)
            h = cot[at, :].astype(jnp.float32)
            p = jax.nn.sigmoid(g)
            hp = h * p
            gate_delta[at, :] = (hp * u * (1.0 + g * (1.0 - p))).astype(jnp.bfloat16)
            up_delta[at, :] = (hp * g).astype(jnp.bfloat16)

    gather_body(n, tok, out, sems, deltas)


def rest_kernel(n, tok, after, out, *sems):
    gather_body(n, tok, out, sems)


def gather_sems(n):
    return [pltpu.SemaphoreType.DMA((n // 2,))] * 4 + [pltpu.SemaphoreType.DMA((1,))]


def first_call(n, tok, gate, up, cot):
    like = jax.ShapeDtypeStruct(gate.shape, jnp.bfloat16)
    return pl.pallas_call(
        partial(first_kernel, n),
        name="first_gather",
        out_shape=(jax.ShapeDtypeStruct((n * tok.shape[0], tok.shape[1]), tok.dtype), like, like),
        in_specs=[VMEM] * 4,
        out_specs=(ANY, VMEM, VMEM),
        scratch_shapes=gather_sems(n),
        compiler_params=pltpu.CompilerParams(collective_id=0, has_side_effects=True),
    )(tok, gate, up, cot)


def rest_call(n, ident, tok, after):
    return pl.pallas_call(
        partial(rest_kernel, n),
        name="rest_gather",
        out_shape=jax.ShapeDtypeStruct((n * tok.shape[0], tok.shape[1]), tok.dtype),
        in_specs=[VMEM, ANY],
        out_specs=ANY,
        scratch_shapes=gather_sems(n),
        compiler_params=pltpu.CompilerParams(collective_id=ident, has_side_effects=True),
        cost_estimate=pl.CostEstimate(flops=0, bytes_accessed=100_000_000, transcendentals=0),
    )(tok, after)


def scatter_kernel(n, term, out, parts, send, recv):
    me = lax.axis_index("fsdp")
    rows = out.shape[0]

    def block(owner):
        return term.at[pl.ds(pl.multiple_of(owner * rows, rows), rows), :]

    greet(me, n)
    own = pltpu.make_async_copy(block(me), parts.at[0], recv.at[0])
    own.start()
    copies = []
    for k in range(1, n):
        peer = lax.rem(me + k, n)
        copy = pltpu.make_async_remote_copy(
            src_ref=block(peer),
            dst_ref=parts.at[k],
            send_sem=send.at[k],
            recv_sem=recv.at[k],
            device_id={"fsdp": peer},
            device_id_type=MESH,
        )
        copy.start()
        copies.append(copy)
    own.wait()
    for copy in copies:
        copy.wait()
    tile = min(16, rows)

    @pl.loop(0, rows // tile)
    def _(i):
        at = pl.ds(pl.multiple_of(i * tile, tile), tile)
        total = parts[0, at, :].astype(jnp.float32)
        for k in range(1, n):
            total = total + parts[k, at, :].astype(jnp.float32)
        out[at, :] = total.astype(out.dtype)


def scatter_call(n, ident, term):
    rows, cols = term.shape[0] // n, term.shape[1]
    return pl.pallas_call(
        partial(scatter_kernel, n),
        name="grad_scatter",
        out_shape=jax.ShapeDtypeStruct((rows, cols), term.dtype),
        in_specs=[ANY],
        out_specs=VMEM,
        scratch_shapes=[
            pltpu.VMEM((n, rows, cols), term.dtype),
            pltpu.SemaphoreType.DMA((n,)),
            pltpu.SemaphoreType.DMA((n,)),
        ],
        compiler_params=pltpu.CompilerParams(collective_id=ident, has_side_effects=True),
        cost_estimate=pl.CostEstimate(flops=0, bytes_accessed=200_000_000, transcendentals=0),
    )(term)


def average(own, peer):
    return 0.5 * (own.astype(jnp.float32) + peer.astype(jnp.float32))


def mix_kernel(first, *refs):
    refs = list(refs)
    parts, rest = refs[:4], refs[4:]
    if first:
        grad = rest.pop(0)
    else:
        rest = rest[3:]
    for at in range(2):
        out = rest.pop(0)
        out[...] = average(parts[2 * at][...], parts[2 * at + 1][...]).astype(out.dtype)
    if first:
        rest.pop(0)[...] = grad[...]


def mix_call(parts, whole, low, tile, grad, mixed=None):
    rows, cols = parts[0].shape
    part = pl.BlockSpec((tile, cols), lambda i: (i, 0))
    held = pl.BlockSpec((tile, cols), lambda i: (low // tile + i, 0))
    first = mixed is None
    out = jax.ShapeDtypeStruct((whole, cols), parts[0].dtype)
    operands, in_specs = list(parts), [part] * 4
    out_shape, out_specs = [out, out], [held, held]
    if first:
        all_of = pl.BlockSpec(grad.shape, lambda i: (0, 0))
        operands.append(grad)
        in_specs.append(all_of)
        out_shape.append(jax.ShapeDtypeStruct(grad.shape, grad.dtype))
        out_specs.append(all_of)
    else:
        operands += [grad, *mixed]
        in_specs += [ANY] * 3
    return pl.pallas_call(
        partial(mix_kernel, first),
        name="mix",
        grid=(rows // tile,),
        out_shape=out_shape,
        in_specs=in_specs,
        out_specs=out_specs,
        input_output_aliases={} if first else {5: 0, 6: 1},
        cost_estimate=pl.CostEstimate(
            flops=4 * rows * cols, bytes_accessed=12 * rows * cols, transcendentals=0
        ),
    )(*operands)


def halves(shard_rows, delta, num, factor):
    total = lax.dot_general(
        shard_rows, delta, (((0,), (0,)), ((), ())), preferred_element_type=jnp.float32
    )
    grad = (factor * total).astype(jnp.bfloat16)
    return (num.astype(jnp.float32) - grad.astype(jnp.float32)).astype(jnp.bfloat16)


def exchange(args, exponent):
    return exchange_at(args, exponent)


def exchange_at(args, exponent):
    tokens, gate_num, up_num, push_weight, gate_delta, up_delta, gate_first, up_first = args
    n = lax.axis_size("fsdp")
    peers = lax.axis_size("rep")
    perm = [(i, (i + (1 << exponent)) % peers) for i in range(peers)]
    depth = tokens.shape[1]
    factor = depth ** (-0.5)
    unit = depth // sum(SPLITS)
    bounds = [0]
    for share in SPLITS:
        bounds.append(bounds[-1] + share * unit)

    def send(value):
        return lax.ppermute(value, "rep", perm)

    own = [(gate_first, up_first)]
    got = [(send(gate_first), send(up_first))]
    rest = rest_call(n, 1 + 2 * exponent, tokens[:, bounds[1] :], gate_first)
    for low, high in zip(bounds[1:-1], bounds[2:]):
        rows = rest[:, low - bounds[1] : high - bounds[1]]
        own.append(
            (
                halves(rows, gate_delta, gate_num[low:high], factor),
                halves(rows, up_delta, up_num[low:high], factor),
            )
        )
        at = len(got)
        got.append((send(own[-1][0]), send(own[-1][1])))
    peer_weight = send(push_weight)
    weight = push_weight[0].astype(jnp.float32)
    gate_point = (gate_num.astype(jnp.float32) / weight).astype(jnp.bfloat16)
    up_point = (up_num.astype(jnp.float32) / weight).astype(jnp.bfloat16)
    contract_cols = (((1,), (1,)), ((), ()))
    term = factor * (
        lax.dot_general(gate_delta, gate_point, contract_cols, preferred_element_type=jnp.float32)
        + lax.dot_general(up_delta, up_point, contract_cols, preferred_element_type=jnp.float32)
    )
    input_grad = scatter_call(n, 2 + 2 * exponent, term.astype(jnp.bfloat16))
    mixed = None
    for at, low in enumerate(bounds[:-1]):
        parts = (own[at][0], got[at][0], own[at][1], got[at][1])
        if at == 0:
            *mixed, grad_out = mix_call(parts, depth, low, unit, input_grad)
        else:
            mixed = mix_call(parts, depth, low, unit, input_grad, mixed)
    weight_next = 0.5 * (push_weight.astype(jnp.float32) + peer_weight.astype(jnp.float32))
    return grad_out, mixed[0][None], mixed[1][None], weight_next


def shards(tokens, gate_saved, up_saved, hidden_grad, gate_num, up_num, push_weight, step):
    n = lax.axis_size("fsdp")
    levels = lax.axis_size("rep").bit_length() - 1
    chosen = step[0] % levels
    depth = tokens.shape[1]
    factor = depth ** (-0.5)
    first = depth // sum(SPLITS) * SPLITS[0]
    rows, gate_delta, up_delta = first_call(
        n, tokens[:, :first], gate_saved, up_saved, hidden_grad
    )
    gate_first = halves(rows, gate_delta, gate_num[0, :first], factor)
    up_first = halves(rows, up_delta, up_num[0, :first], factor)
    args = (
        tokens, gate_num[0], up_num[0], push_weight, gate_delta, up_delta, gate_first, up_first
    )
    branches = [partial(exchange, exponent=exponent) for exponent in range(levels)]
    return lax.switch(chosen, branches, args)


def solution(mesh):
    return jax.shard_map(
        shards,
        mesh=mesh,
        in_specs=(
            P(("rep", "fsdp"), None),
            P("rep", "fsdp"),
            P("rep", "fsdp"),
            P("rep", "fsdp"),
            P("rep", None, "fsdp"),
            P("rep", None, "fsdp"),
            P("rep"),
            P(),
        ),
        out_specs=(
            P(("rep", "fsdp"), None),
            P("rep", None, "fsdp"),
            P("rep", None, "fsdp"),
            P("rep"),
        ),
        check_vma=False,
    )
```

```python
from functools import partial

import jax
import jax.numpy as jnp
from jax import lax
from jax.experimental import pallas as pl
from jax.experimental.pallas import tpu as pltpu
from jax.sharding import PartitionSpec as P


MESH = pl.DeviceIdType.MESH
ANY = pl.BlockSpec(memory_space=pl.ANY)
VMEM = pl.BlockSpec(memory_space=pltpu.VMEM)
SPLITS = (3, 6, 13, 2)
PIECES = 4


def greet(me, n):
    barrier = pltpu.get_barrier_semaphore()
    for k in range(1, n):
        pl.semaphore_signal(
            barrier, inc=1, device_id={"fsdp": lax.rem(me + k, n)}, device_id_type=MESH
        )
    pl.semaphore_wait(barrier, n - 1)


def gather_body(n, tok, out, sems, between=None, later=None):
    send, recv, fsend, frecv, local = sems
    me = lax.axis_index("fsdp")
    rows = tok.shape[0]
    beside = me + 1 - 2 * lax.rem(me, 2)

    def block(owner):
        return out.at[pl.ds(pl.multiple_of(owner * rows, rows), rows), :]

    def remote(src, owner, s, r, target):
        return pltpu.make_async_remote_copy(
            src_ref=src,
            dst_ref=block(owner),
            send_sem=s,
            recv_sem=r,
            device_id={"fsdp": target},
            device_id_type=MESH,
        )

    greet(me, n)
    direct = []
    for k in range(1, n // 2):
        copy = remote(tok, me, send.at[k], recv.at[k], lax.rem(me + 2 * k, n))
        copy.start()
        direct.append(copy)
    near = remote(tok, me, send.at[0], recv.at[0], beside)
    near.start()
    own = pltpu.make_async_copy(tok, block(me), local.at[0])
    own.start()
    if between is not None:
        between()
    relays = []
    for k in range(1, n // 2):
        owner = lax.rem(me + n - 2 * k, n)
        remote(tok, owner, send.at[k], recv.at[k], beside).wait_recv()
        copy = remote(block(owner), owner, fsend.at[k], frecv.at[k], beside)
        copy.start()
        relays.append(copy)
    if later is not None:
        later()
    own.wait()
    near.wait_send()
    remote(tok, beside, send.at[0], recv.at[0], beside).wait_recv()
    for copy in direct:
        copy.wait_send()
    for k in range(1, n // 2):
        relays[k - 1].wait_send()
        owner = lax.rem(beside + n - 2 * k, n)
        remote(tok, owner, fsend.at[k], frecv.at[k], beside).wait_recv()


def first_kernel(
    n, factor, tokens, gate, up, cot, gate_num, up_num,
    gate_delta, up_delta, gate_half, up_half,
    land, turned, acts, grads, nums, load, store, *sems
):
    rows, first = gate.shape[0], gate_half.shape[0]
    piece = rows // PIECES
    tile = min(32, piece)
    columns = min(256, gate.shape[1])
    loads = []
    for c in range(PIECES):
        at = pl.ds(c * piece, piece)
        for which, ref in enumerate((gate, up, cot)):
            copy = pltpu.make_async_copy(ref.at[at, :], acts.at[which, at, :], load.at[which, c])
            copy.start()
            loads.append(copy)
    num_loads = []
    for which, ref in enumerate((gate_num, up_num)):
        copy = pltpu.make_async_copy(
            ref.at[pl.ds(0, first), :], nums.at[which], load.at[3, which]
        )
        copy.start()
        num_loads.append(copy)

    def deltas(pieces):
        for c in pieces:
            for copy in loads[3 * c : 3 * c + 3]:
                copy.wait()

            @pl.loop(0, piece // tile)
            def _(i):
                at = pl.ds(pl.multiple_of(c * piece + i * tile, tile), tile)
                g = acts[0, at, :].astype(jnp.float32)
                u = acts[1, at, :].astype(jnp.float32)
                h = acts[2, at, :].astype(jnp.float32)
                p = jax.nn.sigmoid(g)
                hp = h * p
                grads[0, at, :] = (hp * u * (1.0 + g * (1.0 - p))).astype(jnp.bfloat16)
                grads[1, at, :] = (hp * g).astype(jnp.bfloat16)

    half = PIECES // 2
    gather_body(
        n,
        tokens.at[:, pl.ds(0, first)],
        land,
        sems,
        lambda: deltas(range(half)),
        lambda: deltas(range(half, PIECES)),
    )
    turned[...] = land[...].T
    stores = []
    for which, ref in enumerate((gate_delta, up_delta)):
        copy = pltpu.make_async_copy(grads.at[which], ref, store.at[which])
        copy.start()
        stores.append(copy)
    for which, out in enumerate((gate_half, up_half)):
        num_loads[which].wait()

        @pl.loop(0, gate.shape[1] // columns)
        def _(j):
            at = pl.ds(pl.multiple_of(j * columns, columns), columns)
            total = jnp.dot(turned[...], grads[which, :, at], preferred_element_type=jnp.float32)
            grad = (factor * total).astype(jnp.bfloat16)
            out[:, at] = (
                nums[which, :, at].astype(jnp.float32) - grad.astype(jnp.float32)
            ).astype(jnp.bfloat16)

    for copy in stores:
        copy.wait()


def rest_kernel(n, tok, after, out, *sems):
    gather_body(n, tok, out, sems)


def gather_sems(n):
    return [pltpu.SemaphoreType.DMA((n // 2,))] * 4 + [pltpu.SemaphoreType.DMA((1,))]


def first_call(n, first, factor, tokens, gate, up, cot, gate_num, up_num):
    rows, cols = gate.shape
    delta = jax.ShapeDtypeStruct((rows, cols), jnp.bfloat16)
    half = jax.ShapeDtypeStruct((first, cols), jnp.bfloat16)
    return pl.pallas_call(
        partial(first_kernel, n, factor),
        name="first_gather",
        out_shape=(delta, delta, half, half),
        in_specs=[ANY] * 6,
        out_specs=(ANY, ANY, VMEM, VMEM),
        scratch_shapes=[
            pltpu.VMEM((rows, first), jnp.bfloat16),
            pltpu.VMEM((first, rows), jnp.bfloat16),
            pltpu.VMEM((3, rows, cols), jnp.bfloat16),
            pltpu.VMEM((2, rows, cols), jnp.bfloat16),
            pltpu.VMEM((2, first, cols), jnp.bfloat16),
            pltpu.SemaphoreType.DMA((4, PIECES)),
            pltpu.SemaphoreType.DMA((2,)),
        ]
        + gather_sems(n),
        compiler_params=pltpu.CompilerParams(collective_id=0, has_side_effects=True),
    )(tokens, gate, up, cot, gate_num, up_num)


def rest_call(n, ident, tok, after):
    return pl.pallas_call(
        partial(rest_kernel, n),
        name="rest_gather",
        out_shape=jax.ShapeDtypeStruct((n * tok.shape[0], tok.shape[1]), tok.dtype),
        in_specs=[VMEM, ANY],
        out_specs=ANY,
        scratch_shapes=gather_sems(n),
        compiler_params=pltpu.CompilerParams(collective_id=ident, has_side_effects=True),
        cost_estimate=pl.CostEstimate(flops=0, bytes_accessed=100_000_000, transcendentals=0),
    )(tok, after)


def scatter_kernel(n, term, out, parts, send, recv):
    me = lax.axis_index("fsdp")
    rows = out.shape[0]

    def block(owner):
        return term.at[pl.ds(pl.multiple_of(owner * rows, rows), rows), :]

    greet(me, n)
    own = pltpu.make_async_copy(block(me), parts.at[0], recv.at[0])
    own.start()
    copies = []
    for k in range(1, n):
        peer = lax.rem(me + k, n)
        copy = pltpu.make_async_remote_copy(
            src_ref=block(peer),
            dst_ref=parts.at[k],
            send_sem=send.at[k],
            recv_sem=recv.at[k],
            device_id={"fsdp": peer},
            device_id_type=MESH,
        )
        copy.start()
        copies.append(copy)
    own.wait()
    for copy in copies:
        copy.wait()
    tile = min(16, rows)

    @pl.loop(0, rows // tile)
    def _(i):
        at = pl.ds(pl.multiple_of(i * tile, tile), tile)
        total = parts[0, at, :].astype(jnp.float32)
        for k in range(1, n):
            total = total + parts[k, at, :].astype(jnp.float32)
        out[at, :] = total.astype(out.dtype)


def scatter_call(n, ident, term):
    rows, cols = term.shape[0] // n, term.shape[1]
    return pl.pallas_call(
        partial(scatter_kernel, n),
        name="grad_scatter",
        out_shape=jax.ShapeDtypeStruct((rows, cols), term.dtype),
        in_specs=[ANY],
        out_specs=VMEM,
        scratch_shapes=[
            pltpu.VMEM((n, rows, cols), term.dtype),
            pltpu.SemaphoreType.DMA((n,)),
            pltpu.SemaphoreType.DMA((n,)),
        ],
        compiler_params=pltpu.CompilerParams(collective_id=ident, has_side_effects=True),
        cost_estimate=pl.CostEstimate(flops=0, bytes_accessed=200_000_000, transcendentals=0),
    )(term)


def average(own, peer):
    return 0.5 * (own.astype(jnp.float32) + peer.astype(jnp.float32))


def mix_kernel(first, *refs):
    refs = list(refs)
    parts, rest = refs[:4], refs[4:]
    if first:
        grad = rest.pop(0)
    else:
        rest = rest[3:]
    for at in range(2):
        out = rest.pop(0)
        out[...] = average(parts[2 * at][...], parts[2 * at + 1][...]).astype(out.dtype)
    if first:
        rest.pop(0)[...] = grad[...]


def mix_call(parts, whole, low, tile, grad, mixed=None):
    rows, cols = parts[0].shape
    part = pl.BlockSpec((tile, cols), lambda i: (i, 0))
    held = pl.BlockSpec((tile, cols), lambda i: (low // tile + i, 0))
    first = mixed is None
    out = jax.ShapeDtypeStruct((whole, cols), parts[0].dtype)
    operands, in_specs = list(parts), [part] * 4
    out_shape, out_specs = [out, out], [held, held]
    if first:
        all_of = pl.BlockSpec(grad.shape, lambda i: (0, 0))
        operands.append(grad)
        in_specs.append(all_of)
        out_shape.append(jax.ShapeDtypeStruct(grad.shape, grad.dtype))
        out_specs.append(all_of)
    else:
        operands += [grad, *mixed]
        in_specs += [ANY] * 3
    return pl.pallas_call(
        partial(mix_kernel, first),
        name="mix",
        grid=(rows // tile,),
        out_shape=out_shape,
        in_specs=in_specs,
        out_specs=out_specs,
        input_output_aliases={} if first else {5: 0, 6: 1},
        cost_estimate=pl.CostEstimate(
            flops=4 * rows * cols, bytes_accessed=12 * rows * cols, transcendentals=0
        ),
    )(*operands)


def halves(shard_rows, delta, num, factor):
    total = lax.dot_general(
        shard_rows, delta, (((0,), (0,)), ((), ())), preferred_element_type=jnp.float32
    )
    grad = (factor * total).astype(jnp.bfloat16)
    return (num.astype(jnp.float32) - grad.astype(jnp.float32)).astype(jnp.bfloat16)


def exchange(args, exponent):
    return exchange_at(args, exponent)


def exchange_at(args, exponent):
    tokens, gate_num, up_num, push_weight, gate_delta, up_delta, gate_first, up_first = args
    n = lax.axis_size("fsdp")
    peers = lax.axis_size("rep")
    perm = [(i, (i + (1 << exponent)) % peers) for i in range(peers)]
    depth = tokens.shape[1]
    factor = depth ** (-0.5)
    unit = depth // sum(SPLITS)
    bounds = [0]
    for share in SPLITS:
        bounds.append(bounds[-1] + share * unit)

    def send(value):
        return lax.ppermute(value, "rep", perm)

    own = [(gate_first, up_first)]
    got = [(send(gate_first), send(up_first))]
    rest = rest_call(n, 1 + 2 * exponent, tokens[:, bounds[1] :], gate_first)
    for low, high in zip(bounds[1:-1], bounds[2:]):
        rows = rest[:, low - bounds[1] : high - bounds[1]]
        own.append(
            (
                halves(rows, gate_delta, gate_num[low:high], factor),
                halves(rows, up_delta, up_num[low:high], factor),
            )
        )
        at = len(got)
        got.append((send(own[-1][0]), send(own[-1][1])))
    peer_weight = send(push_weight)
    weight = push_weight[0].astype(jnp.float32)
    gate_point = (gate_num.astype(jnp.float32) / weight).astype(jnp.bfloat16)
    up_point = (up_num.astype(jnp.float32) / weight).astype(jnp.bfloat16)
    contract_cols = (((1,), (1,)), ((), ()))
    term = factor * (
        lax.dot_general(gate_delta, gate_point, contract_cols, preferred_element_type=jnp.float32)
        + lax.dot_general(up_delta, up_point, contract_cols, preferred_element_type=jnp.float32)
    )
    input_grad = scatter_call(n, 2 + 2 * exponent, term.astype(jnp.bfloat16))
    mixed = None
    for at, low in enumerate(bounds[:-1]):
        parts = (own[at][0], got[at][0], own[at][1], got[at][1])
        if at == 0:
            *mixed, grad_out = mix_call(parts, depth, low, unit, input_grad)
        else:
            mixed = mix_call(parts, depth, low, unit, input_grad, mixed)
    weight_next = 0.5 * (push_weight.astype(jnp.float32) + peer_weight.astype(jnp.float32))
    return grad_out, mixed[0][None], mixed[1][None], weight_next


def shards(tokens, gate_saved, up_saved, hidden_grad, gate_num, up_num, push_weight, step):
    n = lax.axis_size("fsdp")
    levels = lax.axis_size("rep").bit_length() - 1
    chosen = step[0] % levels
    depth = tokens.shape[1]
    factor = depth ** (-0.5)
    first = depth // sum(SPLITS) * SPLITS[0]
    gate_delta, up_delta, gate_first, up_first = first_call(
        n, first, factor, tokens, gate_saved, up_saved, hidden_grad, gate_num[0], up_num[0]
    )
    args = (
        tokens, gate_num[0], up_num[0], push_weight, gate_delta, up_delta, gate_first, up_first
    )
    branches = [partial(exchange, exponent=exponent) for exponent in range(levels)]
    return lax.switch(chosen, branches, args)


def solution(mesh):
    return jax.shard_map(
        shards,
        mesh=mesh,
        in_specs=(
            P(("rep", "fsdp"), None),
            P("rep", "fsdp"),
            P("rep", "fsdp"),
            P("rep", "fsdp"),
            P("rep", None, "fsdp"),
            P("rep", None, "fsdp"),
            P("rep"),
            P(),
        ),
        out_specs=(
            P(("rep", "fsdp"), None),
            P("rep", None, "fsdp"),
            P("rep", None, "fsdp"),
            P("rep"),
        ),
        check_vma=False,
    )
```

```python
from functools import partial

import jax
import jax.numpy as jnp
from jax import lax
from jax.experimental import pallas as pl
from jax.experimental.pallas import tpu as pltpu
from jax.sharding import PartitionSpec as P


MESH = pl.DeviceIdType.MESH
ANY = pl.BlockSpec(memory_space=pl.ANY)
VMEM = pl.BlockSpec(memory_space=pltpu.VMEM)
SPLITS = (3, 5, 14, 2)
PIECES = 4


def greet(me, n):
    barrier = pltpu.get_barrier_semaphore()
    for k in range(1, n):
        pl.semaphore_signal(
            barrier, inc=1, device_id={"fsdp": lax.rem(me + k, n)}, device_id_type=MESH
        )
    pl.semaphore_wait(barrier, n - 1)


def gather_body(n, tok, out, sems, between=None, later=None):
    send, recv, fsend, frecv, local = sems
    me = lax.axis_index("fsdp")
    rows = tok.shape[0]
    beside = me + 1 - 2 * lax.rem(me, 2)

    def block(owner):
        return out.at[pl.ds(pl.multiple_of(owner * rows, rows), rows), :]

    def remote(src, owner, s, r, target):
        return pltpu.make_async_remote_copy(
            src_ref=src,
            dst_ref=block(owner),
            send_sem=s,
            recv_sem=r,
            device_id={"fsdp": target},
            device_id_type=MESH,
        )

    greet(me, n)
    direct = []
    for k in range(1, n // 2):
        copy = remote(tok, me, send.at[k], recv.at[k], lax.rem(me + 2 * k, n))
        copy.start()
        direct.append(copy)
    near = remote(tok, me, send.at[0], recv.at[0], beside)
    near.start()
    own = pltpu.make_async_copy(tok, block(me), local.at[0])
    own.start()
    if between is not None:
        between()
    relays = []
    for k in range(1, n // 2):
        owner = lax.rem(me + n - 2 * k, n)
        remote(tok, owner, send.at[k], recv.at[k], beside).wait_recv()
        copy = remote(block(owner), owner, fsend.at[k], frecv.at[k], beside)
        copy.start()
        relays.append(copy)
    if later is not None:
        later()
    own.wait()
    near.wait_send()
    remote(tok, beside, send.at[0], recv.at[0], beside).wait_recv()
    for copy in direct:
        copy.wait_send()
    for k in range(1, n // 2):
        relays[k - 1].wait_send()
        owner = lax.rem(beside + n - 2 * k, n)
        remote(tok, owner, fsend.at[k], frecv.at[k], beside).wait_recv()


def first_kernel(
    n, factor, tokens, gate, up, cot, gate_num, up_num,
    gate_delta, up_delta, gate_half, up_half,
    land, turned, acts, grads, nums, load, store, *sems
):
    rows, first = gate.shape[0], gate_half.shape[0]
    piece = rows // PIECES
    tile = min(32, piece)
    columns = min(256, gate.shape[1])
    loads = []
    for c in range(PIECES):
        at = pl.ds(c * piece, piece)
        for which, ref in enumerate((gate, up, cot)):
            copy = pltpu.make_async_copy(ref.at[at, :], acts.at[which, at, :], load.at[which, c])
            copy.start()
            loads.append(copy)
    num_loads = []
    for which, ref in enumerate((gate_num, up_num)):
        copy = pltpu.make_async_copy(
            ref.at[pl.ds(0, first), :], nums.at[which], load.at[3, which]
        )
        copy.start()
        num_loads.append(copy)

    def deltas(pieces):
        for c in pieces:
            for copy in loads[3 * c : 3 * c + 3]:
                copy.wait()

            @pl.loop(0, piece // tile)
            def _(i):
                at = pl.ds(pl.multiple_of(c * piece + i * tile, tile), tile)
                g = acts[0, at, :].astype(jnp.float32)
                u = acts[1, at, :].astype(jnp.float32)
                h = acts[2, at, :].astype(jnp.float32)
                p = jax.nn.sigmoid(g)
                hp = h * p
                grads[0, at, :] = (hp * u * (1.0 + g * (1.0 - p))).astype(jnp.bfloat16)
                grads[1, at, :] = (hp * g).astype(jnp.bfloat16)

    half = PIECES // 2
    gather_body(
        n,
        tokens.at[:, pl.ds(0, first)],
        land,
        sems,
        lambda: deltas(range(half)),
        lambda: deltas(range(half, PIECES)),
    )
    turned[...] = land[...].T
    stores = []
    for which, ref in enumerate((gate_delta, up_delta)):
        copy = pltpu.make_async_copy(grads.at[which], ref, store.at[which])
        copy.start()
        stores.append(copy)
    for which, out in enumerate((gate_half, up_half)):
        num_loads[which].wait()

        @pl.loop(0, gate.shape[1] // columns)
        def _(j):
            at = pl.ds(pl.multiple_of(j * columns, columns), columns)
            total = jnp.dot(turned[...], grads[which, :, at], preferred_element_type=jnp.float32)
            grad = (factor * total).astype(jnp.bfloat16)
            out[:, at] = (
                nums[which, :, at].astype(jnp.float32) - grad.astype(jnp.float32)
            ).astype(jnp.bfloat16)

    for copy in stores:
        copy.wait()


def rest_kernel(n, tok, after, out, *sems):
    gather_body(n, tok, out, sems)


def gather_sems(n):
    return [pltpu.SemaphoreType.DMA((n // 2,))] * 4 + [pltpu.SemaphoreType.DMA((1,))]


def first_call(n, first, factor, tokens, gate, up, cot, gate_num, up_num):
    rows, cols = gate.shape
    delta = jax.ShapeDtypeStruct((rows, cols), jnp.bfloat16)
    half = jax.ShapeDtypeStruct((first, cols), jnp.bfloat16)
    return pl.pallas_call(
        partial(first_kernel, n, factor),
        name="first_gather",
        out_shape=(delta, delta, half, half),
        in_specs=[ANY] * 6,
        out_specs=(ANY, ANY, VMEM, VMEM),
        scratch_shapes=[
            pltpu.VMEM((rows, first), jnp.bfloat16),
            pltpu.VMEM((first, rows), jnp.bfloat16),
            pltpu.VMEM((3, rows, cols), jnp.bfloat16),
            pltpu.VMEM((2, rows, cols), jnp.bfloat16),
            pltpu.VMEM((2, first, cols), jnp.bfloat16),
            pltpu.SemaphoreType.DMA((4, PIECES)),
            pltpu.SemaphoreType.DMA((2,)),
        ]
        + gather_sems(n),
        compiler_params=pltpu.CompilerParams(collective_id=0, has_side_effects=True),
    )(tokens, gate, up, cot, gate_num, up_num)


def rest_call(n, ident, tok, after):
    return pl.pallas_call(
        partial(rest_kernel, n),
        name="rest_gather",
        out_shape=jax.ShapeDtypeStruct((n * tok.shape[0], tok.shape[1]), tok.dtype),
        in_specs=[VMEM, ANY],
        out_specs=ANY,
        scratch_shapes=gather_sems(n),
        compiler_params=pltpu.CompilerParams(collective_id=ident, has_side_effects=True),
        cost_estimate=pl.CostEstimate(flops=0, bytes_accessed=100_000_000, transcendentals=0),
    )(tok, after)


def scatter_kernel(n, term, out, parts, send, recv):
    me = lax.axis_index("fsdp")
    rows = out.shape[0]

    def block(owner):
        return term.at[pl.ds(pl.multiple_of(owner * rows, rows), rows), :]

    greet(me, n)
    own = pltpu.make_async_copy(block(me), parts.at[0], recv.at[0])
    own.start()
    copies = []
    for k in range(1, n):
        peer = lax.rem(me + k, n)
        copy = pltpu.make_async_remote_copy(
            src_ref=block(peer),
            dst_ref=parts.at[k],
            send_sem=send.at[k],
            recv_sem=recv.at[k],
            device_id={"fsdp": peer},
            device_id_type=MESH,
        )
        copy.start()
        copies.append(copy)
    own.wait()
    for copy in copies:
        copy.wait()
    tile = min(16, rows)

    @pl.loop(0, rows // tile)
    def _(i):
        at = pl.ds(pl.multiple_of(i * tile, tile), tile)
        total = parts[0, at, :].astype(jnp.float32)
        for k in range(1, n):
            total = total + parts[k, at, :].astype(jnp.float32)
        out[at, :] = total.astype(out.dtype)


def scatter_call(n, ident, term):
    rows, cols = term.shape[0] // n, term.shape[1]
    return pl.pallas_call(
        partial(scatter_kernel, n),
        name="grad_scatter",
        out_shape=jax.ShapeDtypeStruct((rows, cols), term.dtype),
        in_specs=[ANY],
        out_specs=VMEM,
        scratch_shapes=[
            pltpu.VMEM((n, rows, cols), term.dtype),
            pltpu.SemaphoreType.DMA((n,)),
            pltpu.SemaphoreType.DMA((n,)),
        ],
        compiler_params=pltpu.CompilerParams(collective_id=ident, has_side_effects=True),
        cost_estimate=pl.CostEstimate(flops=0, bytes_accessed=200_000_000, transcendentals=0),
    )(term)


def average(own, peer):
    return 0.5 * (own.astype(jnp.float32) + peer.astype(jnp.float32))


def mix_kernel(first, *refs):
    refs = list(refs)
    parts, rest = refs[:4], refs[4:]
    if first:
        grad = rest.pop(0)
    else:
        rest = rest[3:]
    for at in range(2):
        out = rest.pop(0)
        out[...] = average(parts[2 * at][...], parts[2 * at + 1][...]).astype(out.dtype)
    if first:
        rest.pop(0)[...] = grad[...]


def mix_call(parts, whole, low, tile, grad, mixed=None):
    rows, cols = parts[0].shape
    part = pl.BlockSpec((tile, cols), lambda i: (i, 0))
    held = pl.BlockSpec((tile, cols), lambda i: (low // tile + i, 0))
    first = mixed is None
    out = jax.ShapeDtypeStruct((whole, cols), parts[0].dtype)
    operands, in_specs = list(parts), [part] * 4
    out_shape, out_specs = [out, out], [held, held]
    if first:
        all_of = pl.BlockSpec(grad.shape, lambda i: (0, 0))
        operands.append(grad)
        in_specs.append(all_of)
        out_shape.append(jax.ShapeDtypeStruct(grad.shape, grad.dtype))
        out_specs.append(all_of)
    else:
        operands += [grad, *mixed]
        in_specs += [ANY] * 3
    return pl.pallas_call(
        partial(mix_kernel, first),
        name="mix",
        grid=(rows // tile,),
        out_shape=out_shape,
        in_specs=in_specs,
        out_specs=out_specs,
        input_output_aliases={} if first else {5: 0, 6: 1},
        cost_estimate=pl.CostEstimate(
            flops=4 * rows * cols, bytes_accessed=12 * rows * cols, transcendentals=0
        ),
    )(*operands)


def halves(shard_rows, delta, num, factor):
    total = lax.dot_general(
        shard_rows, delta, (((0,), (0,)), ((), ())), preferred_element_type=jnp.float32
    )
    grad = (factor * total).astype(jnp.bfloat16)
    return (num.astype(jnp.float32) - grad.astype(jnp.float32)).astype(jnp.bfloat16)


def exchange(args, exponent):
    return exchange_at(args, exponent)


def exchange_at(args, exponent):
    tokens, gate_num, up_num, push_weight, gate_delta, up_delta, gate_first, up_first = args
    n = lax.axis_size("fsdp")
    peers = lax.axis_size("rep")
    perm = [(i, (i + (1 << exponent)) % peers) for i in range(peers)]
    depth = tokens.shape[1]
    factor = depth ** (-0.5)
    unit = depth // sum(SPLITS)
    bounds = [0]
    for share in SPLITS:
        bounds.append(bounds[-1] + share * unit)

    def send(value):
        return lax.ppermute(value, "rep", perm)

    own = [(gate_first, up_first)]
    got = [(send(gate_first), send(up_first))]
    for low, high in zip(bounds[1:-1], bounds[2:]):
        if len(got) == 1:
            start, rest = low, rest_call(n, 1 + 3 * exponent, tokens[:, low:high], up_first)
        elif len(got) == 2:
            start, rest = low, rest_call(n, 2 + 3 * exponent, tokens[:, low:], own[-1][1])
        rows = rest[:, low - start : high - start]
        own.append(
            (
                halves(rows, gate_delta, gate_num[low:high], factor),
                halves(rows, up_delta, up_num[low:high], factor),
            )
        )
        at = len(got)
        got.append((send(own[-1][0]), send(own[-1][1])))
    peer_weight = send(push_weight)
    weight = push_weight[0].astype(jnp.float32)
    gate_point = (gate_num.astype(jnp.float32) / weight).astype(jnp.bfloat16)
    up_point = (up_num.astype(jnp.float32) / weight).astype(jnp.bfloat16)
    contract_cols = (((1,), (1,)), ((), ()))
    term = factor * (
        lax.dot_general(gate_delta, gate_point, contract_cols, preferred_element_type=jnp.float32)
        + lax.dot_general(up_delta, up_point, contract_cols, preferred_element_type=jnp.float32)
    )
    input_grad = scatter_call(n, 3 + 3 * exponent, term.astype(jnp.bfloat16))
    mixed = None
    for at, low in enumerate(bounds[:-1]):
        parts = (own[at][0], got[at][0], own[at][1], got[at][1])
        if at == 0:
            *mixed, grad_out = mix_call(parts, depth, low, unit, input_grad)
        else:
            mixed = mix_call(parts, depth, low, unit, input_grad, mixed)
    weight_next = 0.5 * (push_weight.astype(jnp.float32) + peer_weight.astype(jnp.float32))
    return grad_out, mixed[0][None], mixed[1][None], weight_next


def shards(tokens, gate_saved, up_saved, hidden_grad, gate_num, up_num, push_weight, step):
    n = lax.axis_size("fsdp")
    levels = lax.axis_size("rep").bit_length() - 1
    chosen = step[0] % levels
    depth = tokens.shape[1]
    factor = depth ** (-0.5)
    first = depth // sum(SPLITS) * SPLITS[0]
    gate_delta, up_delta, gate_first, up_first = first_call(
        n, first, factor, tokens, gate_saved, up_saved, hidden_grad, gate_num[0], up_num[0]
    )
    args = (
        tokens, gate_num[0], up_num[0], push_weight, gate_delta, up_delta, gate_first, up_first
    )
    branches = [partial(exchange, exponent=exponent) for exponent in range(levels)]
    return lax.switch(chosen, branches, args)


def solution(mesh):
    return jax.shard_map(
        shards,
        mesh=mesh,
        in_specs=(
            P(("rep", "fsdp"), None),
            P("rep", "fsdp"),
            P("rep", "fsdp"),
            P("rep", "fsdp"),
            P("rep", None, "fsdp"),
            P("rep", None, "fsdp"),
            P("rep"),
            P(),
        ),
        out_specs=(
            P(("rep", "fsdp"), None),
            P("rep", None, "fsdp"),
            P("rep", None, "fsdp"),
            P("rep"),
        ),
        check_vma=False,
    )
```
